32 devices in a mesh: rows: 16 (over z, y, x), cols: 2 (over core).
Axes of the slice: x: 2, y: 2, z: 4, core: 2. Of those that a mesh axis runs over, the one named last changes fastest.
Arguments:
- parent_front: float32 [4096, 2048], P('rows', 'cols')
- right_sides: float32 [4096, 64], P('rows'), may hold values from -6 to 6
- child_values: float32 [1024, 1024], P('rows', 'cols'), may hold values from -6 to 6
- block_owner: int32 [256], P('rows'), may hold values from 0 to 15, as said below
- row_map: int32 [1024], P('rows'), may hold values from 0 to 255
- col_map: int32 [1024], P('cols'), may hold values from 0 to 1023, as said below
Outputs:
- updated: float32 [4096, 2048], P('rows', 'cols')
- side_coeffs: float32 [128, 64], replicated
- side_left: float32 [4096, 64], P('rows')
The draws below stay inside these ranges and needn't reach their ends.
Inputs may be any that keep to these rules, and one draw needn't show every extreme that they name: `block_owner`: for every k, entries k * 16 to (k + 1) * 16 - 1 form a permutation of 0 to 15. `col_map`: each aligned run of 512 entries is strictly increasing, starts with 0 and ends with 1023.
All inputs are finite; a program needn't handle non-finite values.
Results may differ from the reference program's by a relative error of at most 0.0003.
Values sent between devices are 32-bit elements; how exact they have to be, the bound alone decides.
A program may use at most 64 MiB of HBM per device.

```python
import math
import jax
import jax.numpy as jnp
from jax import lax

R_DEV = 256
C_DEV = 1024
PANEL = 128
RHS = 64
RBLOCKS = 16
NR = 4096
NC = 2048
BLK = 4
CH_ROWS = 1024
CC_DEV = 512
CHC = 1024


def draw_parent_front(key, part):
    keys = jax.random.split(key, 3)
    entries = jax.random.normal(keys[0], (NR, NC), jnp.float32)
    trailing = (jnp.arange(NC) >= PANEL).astype(jnp.float32)[None, :]
    rising = jnp.exp(math.log(3.0) * jnp.arange(NR, dtype=jnp.float32) / NR)[:, None]
    row_scale = 0.4 * jnp.exp(math.log(10.0) * jax.random.uniform(keys[1], (NR, 1), jnp.float32)) * rising
    col_spread = 0.3 * jnp.exp(math.log(10.0) * jax.random.uniform(keys[2], (1, NC), jnp.float32))
    col_scale = trailing * col_spread + (1.0 - trailing)
    return entries * row_scale * col_scale


def draw_block_owner(key, part):
    keys = jax.random.split(jax.random.fold_in(key, 11), RBLOCKS)
    table = jax.vmap(lambda single: jax.random.permutation(single, RBLOCKS))(keys)
    return table.reshape(-1).astype(jnp.int32)


def single_map(key):
    chosen = jax.random.permutation(key, C_DEV - 2)[:CC_DEV - 2] + 1
    inner = jnp.sort(chosen).astype(jnp.int32)
    first = jnp.zeros((1,), jnp.int32)
    final = jnp.full((1,), C_DEV - 1, jnp.int32)
    return jnp.concatenate([first, inner, final])


def draw_col_map(key, part):
    keys = jax.random.split(jax.random.fold_in(key, 23), CHC // CC_DEV)
    return jax.vmap(single_map)(keys).reshape(-1).astype(jnp.int32)


def with_ends(values, stream_key, least, largest):
    dims = values.shape
    spot = [jax.random.randint(jax.random.fold_in(stream_key, axis), (), 0, dims[axis]) for axis in range(len(dims))]
    values = values.at[tuple(spot)].set(least)
    longest = dims.index(max(dims))
    spot[longest] = (spot[longest] + 1) % dims[longest]
    return values.at[tuple(spot)].set(largest)


def block_scale(own_key, shape, cuts, smallest, largest):
    factor_of, own = 1.0, jax.random.fold_in(own_key, 6)
    for axis_at, blocks in cuts:
        heights = jnp.exp(jax.random.uniform(jax.random.fold_in(own, axis_at), (blocks,), jnp.float32, smallest / len(cuts), largest / len(cuts)))
        factor_of = factor_of * jnp.repeat(heights, shape[axis_at] // blocks).reshape([-1 if axis == axis_at else 1 for axis in range(len(shape))])
    return factor_of


def bell_draw(stream_key, shape, width, bound, shards=(), kind=jnp.bfloat16):
    result = width * jax.random.normal(stream_key, shape, jnp.float32)
    if shards:
        result = result * block_scale(stream_key, shape, shards, -0.22, 0.18)
    return jnp.clip(result, -bound, bound).astype(kind)


def setup_inputs(seed: int = 0) -> dict:
    key_list = jax.random.split(jax.random.key(seed), 7)
    return {
        "parent_front": draw_parent_front(jax.random.fold_in(key_list[6], 71), 0),
        "right_sides": bell_draw(key_list[1], (NR, RHS), 1.0, 6.0, ((0, 16),), jnp.float32),
        "child_values": bell_draw(key_list[2], (CH_ROWS, CHC), 1.0, 6.0, ((0, 16), (1, 2)), jnp.float32),
        "block_owner": draw_block_owner(jax.random.fold_in(key_list[6], 71), 0),
        "row_map": with_ends(jax.random.randint(key_list[4], (CH_ROWS,), 0, R_DEV), jax.random.fold_in(key_list[4], 1), 0, R_DEV - 1).astype(jnp.int32),
        "col_map": draw_col_map(jax.random.fold_in(key_list[6], 71), 0),
    }


def reference(parent_front, right_sides, child_values, block_owner, row_map, col_map):
    child_index = jnp.arange(CH_ROWS, dtype=jnp.int32)
    parent_row = (block_owner[child_index // BLK] * R_DEV + row_map).astype(jnp.int32)
    column_index = jnp.arange(CHC, dtype=jnp.int32)
    parent_col = (column_index // CC_DEV * C_DEV + col_map).astype(jnp.int32)
    assembled = parent_front.at[parent_row[:, None], parent_col[None, :]].add(child_values)
    panel_rows = assembled[:, :PANEL]
    orthogonal, upper = jnp.linalg.qr(panel_rows)
    projected = jnp.dot(orthogonal.T, assembled, precision=lax.Precision.HIGHEST)
    coefs = jax.scipy.linalg.solve_triangular(upper, projected, lower=False)
    updated = assembled - jnp.dot(panel_rows, coefs, precision=lax.Precision.HIGHEST)
    side_projected = jnp.dot(orthogonal.T, right_sides, precision=lax.Precision.HIGHEST)
    side_coeffs = jax.scipy.linalg.solve_triangular(upper, side_projected, lower=False)
    side_left = right_sides - jnp.dot(panel_rows, side_coeffs, precision=lax.Precision.HIGHEST)
    return (updated, side_coeffs, side_left)
```

```python
import functools

import jax
import jax.numpy as jnp
from jax import lax
from jax.experimental import pallas as pl
from jax.experimental.pallas import tpu as pltpu
from jax.sharding import PartitionSpec as P

PANEL = 128
LANES = 128
SUBLANES = 8
MESH = pl.DeviceIdType.MESH
f32 = jnp.float32
bf16 = jnp.bfloat16


def pieces(value):
    first = value.astype(bf16)
    rest = value - first.astype(f32)
    second = rest.astype(bf16)
    third = (rest - second.astype(f32)).astype(bf16)
    return first, second, third


def dot(left, right, dims, precision=None):
    return lax.dot_general(left, right, (dims, ((), ())), precision=precision, preferred_element_type=f32)


def dot_full(left, right, dims=((1,), (0,))):
    return dot(left, right, dims, lax.Precision.HIGHEST)


def sweep_pair(mat, k, lane, sub):
    row0, row1 = mat[k : k + 1, :], mat[k + 1 : k + 2, :]
    col0, col1 = mat[:, k : k + 1], mat[:, k + 1 : k + 2]
    a, b, d = mat[k : k + 1, k : k + 1], mat[k : k + 1, k + 1 : k + 2], mat[k + 1 : k + 2, k + 1 : k + 2]
    ia = 1.0 / a
    ratio = b * ia
    i11 = 1.0 / (d - b * ratio)
    i01 = -ratio * i11
    i00 = ia - ratio * i01
    top0, top1 = i00 * row0 + i01 * row1, i01 * row0 + i11 * row1
    side0, side1 = i00 * col0 + i01 * col1, i01 * col0 + i11 * col1
    lane_row = lane[:1]
    top0 = jnp.where(lane_row == k, -i00, jnp.where(lane_row == k + 1, -i01, top0))
    top1 = jnp.where(lane_row == k, -i01, jnp.where(lane_row == k + 1, -i11, top1))
    raw0 = i00 * row0 + i01 * row1
    raw1 = i01 * row0 + i11 * row1
    out = mat - col0 * raw0 - col1 * raw1
    out = jnp.where(lane == k, side0, jnp.where(lane == k + 1, side1, out))
    out = jnp.where(sub == k, top0, jnp.where(sub == k + 1, top1, out))
    return out


def inverse_of(gram):
    size = gram.shape[0]
    lane = lax.broadcasted_iota(jnp.int32, gram.shape, 1)
    sub = lax.broadcasted_iota(jnp.int32, gram.shape, 0)

    def group(_, mat):
        for k in range(0, SUBLANES, 2):
            mat = sweep_pair(mat, k, lane, sub)
        mat = jnp.concatenate([mat[SUBLANES:], mat[:SUBLANES]], axis=0)
        return pltpu.roll(mat, size - SUBLANES, 1)

    return -lax.fori_loop(0, size // SUBLANES, group, gram)


def kernel(n, ncols, owner, parent, rhs, child, row_map, col_map, updated, side_coeffs, side_left,
           front, send, recv, flat, hot, panel, prod, total, halves, in_sem, a2a_send, a2a_recv, pan_send, pan_recv,
           red_send, red_recv):
    row, col = lax.axis_index("rows"), lax.axis_index("cols")
    rows_dev, cols_dev = front.shape
    child_rows, child_cols = child.shape
    block = child_rows // n
    levels = n.bit_length() - 1
    load = pltpu.make_async_copy(parent, front, in_sem)
    load.start()

    barrier = pltpu.get_barrier_semaphore()
    for step in range(1, n):
        pl.semaphore_signal(barrier, inc=1, device_id=(lax.rem(row + step, n), col), device_id_type=MESH)
    for step in range(1, ncols):
        pl.semaphore_signal(barrier, inc=1, device_id=(row, lax.rem(col + step, ncols)), device_id_type=MESH)

    source = lax.broadcasted_iota(jnp.int32, (1, child_rows), 1)
    target = jnp.zeros((1, child_rows), jnp.int32)
    for k in range(n):
        target = jnp.where(source // block == k, owner[k] * block + source % block, target)
    place = lax.broadcasted_iota(jnp.int32, (child_rows, child_rows), 0) == target
    place_f = jnp.where(place, 1.0, 0.0).astype(f32)
    landing = jnp.sum(place_f * row_map[...].astype(f32), axis=1, keepdims=True)
    place_b = place_f.astype(bf16)
    one, two, three = pieces(child[...])
    ordered = dot(place_b, one, ((1,), (0,))) + dot(place_b, two, ((1,), (0,))) + dot(place_b, three, ((1,), (0,)))
    landing = jnp.broadcast_to(landing, (child_rows, LANES))
    for k in range(n):
        send[k, :, :child_cols] = ordered[k * block : (k + 1) * block]
        send[k, :, child_cols:] = landing[k * block : (k + 1) * block]

    pl.semaphore_wait(barrier, n - 1 + ncols - 1)

    copies = []
    for step in range(1, n):
        peer = lax.rem(row + step, n)
        copy = pltpu.make_async_remote_copy(
            src_ref=send.at[peer], dst_ref=recv.at[row], send_sem=a2a_send.at[step], recv_sem=a2a_recv.at[step],
            device_id=(peer, col), device_id_type=MESH)
        copy.start()
        copies.append(copy)
    recv[row] = send[row]

    cols_at = lax.broadcasted_iota(jnp.int32, hot.shape, 0)
    hot[...] = jnp.where(cols_at == col_map[...], 1.0, 0.0).astype(f32).astype(bf16)
    rhs_pad = prod.shape[1] - cols_dev - PANEL
    load.wait()
    for copy in copies:
        copy.wait()

    for k in range(n):
        flat[k * block : (k + 1) * block, :] = recv[k]
    vals = jnp.concatenate(pieces(flat[:, :child_cols]), axis=0)
    spread3 = dot(vals, hot[...], ((1,), (1,)))
    spread = spread3[:child_rows] + spread3[child_rows : 2 * child_rows] + spread3[2 * child_rows :]
    where_rows = flat[:, child_cols:].astype(jnp.int32)
    rows_at = lax.broadcasted_iota(jnp.int32, where_rows.shape, 1)
    landed = jnp.concatenate(
        [jnp.where(where_rows == rows_at + t * LANES, 1.0, 0.0).astype(f32) for t in range(rows_dev // LANES)], axis=1)
    landed3 = jnp.concatenate([landed] * 3, axis=0).astype(bf16)
    stacked = jnp.concatenate(pieces(spread), axis=0)
    front[...] = front[...] + dot(landed3, stacked, ((0,), (0,)))

    pan_copies = [
        pltpu.make_async_remote_copy(
            src_ref=front.at[:, pl.ds(0, PANEL)], dst_ref=panel, send_sem=pan_send.at[step - 1], recv_sem=pan_recv,
            device_id=(row, step), device_id_type=MESH)
        for step in range(1, ncols)
    ]

    @pl.when(col == 0)
    def _():
        for copy in pan_copies:
            copy.start()
        panel[...] = front[:, :PANEL]
        for copy in pan_copies:
            copy.wait_send()

    @pl.when(col != 0)
    def _():
        pan_copies[0].wait_recv()

    block_panel = panel[...]
    trans = ((0,), (0,))
    prod[:, :cols_dev] = dot_full(block_panel, front[...], trans)
    prod[:, cols_dev : cols_dev + PANEL] = dot_full(block_panel, block_panel, trans)
    sides = jnp.concatenate([rhs[...], jnp.zeros((rows_dev, rhs_pad - rhs.shape[1]), f32)], axis=1)
    prod[:, cols_dev + PANEL :] = dot_full(block_panel, sides, trans)

    tiles = prod.shape[1] // LANES
    nparts = halves.shape[0]
    starts = [tiles * q // nparts * LANES for q in range(nparts + 1)]
    halving = min(levels, (PANEL // SUBLANES).bit_length() - 1)
    lead = min(nparts, levels)
    orders = [[(q + t) % lead for t in range(lead)] + list(range(lead, levels)) for q in range(nparts)]
    base = [jnp.int32(0)] * nparts
    history = [[] for _ in range(nparts)]
    for level in range(levels):
        size = PANEL >> min(level, halving)
        half = size // 2 if level < halving else size
        stage = []
        for q in range(nparts):
            bit = orders[q][level]
            own = (row // (1 << bit)) % 2
            peer = row + (1 - 2 * own) * (1 << bit)
            history[q].append((base[q], own, peer))
            if level < halving:
                keep, give = base[q] + own * half, base[q] + (1 - own) * half
            else:
                keep = give = base[q]
            keep, give = pl.multiple_of(keep, SUBLANES), pl.multiple_of(give, SUBLANES)
            width = starts[q + 1] - starts[q]
            at = sum(
                (PANEL >> (t + 1)) if t < halving else SUBLANES for t in range(level))
            landing_ref = halves.at[q, pl.ds(at, half), pl.ds(0, width)]
            copy = pltpu.make_async_remote_copy(
                src_ref=prod.at[pl.ds(give, half), pl.ds(starts[q], width)], dst_ref=landing_ref,
                send_sem=red_send.at[q, level], recv_sem=red_recv.at[q, level],
                device_id=(peer, col), device_id_type=MESH)
            copy.start()
            stage.append((copy, keep, at, width))
            base[q] = keep
        for q, (copy, keep, at, width) in enumerate(stage):
            copy.wait()
            spot = (pl.ds(keep, half), slice(starts[q], starts[q + 1]))
            prod[spot] = prod[spot] + halves[q, at : at + half, :width]
    size = PANEL >> halving
    for q in range(nparts):
        spot = (pl.ds(base[q], size), slice(starts[q], starts[q + 1]))
        total[spot] = prod[spot]
    for level in reversed(range(halving)):
        size = PANEL >> (level + 1)
        stage = []
        for q in range(nparts):
            older, own, peer = history[q][level]
            keep = pl.multiple_of(older + own * size, SUBLANES)
            spot = total.at[pl.ds(keep, size), pl.ds(starts[q], starts[q + 1] - starts[q])]
            copy = pltpu.make_async_remote_copy(
                src_ref=spot, dst_ref=spot,
                send_sem=red_send.at[q, levels + level], recv_sem=red_recv.at[q, levels + level],
                device_id=(peer, col), device_id_type=MESH)
            copy.start()
            stage.append(copy)
        for copy in stage:
            copy.wait()

    inverse = inverse_of(total[:, cols_dev : cols_dev + PANEL])
    side = dot_full(inverse, total[:, cols_dev + PANEL :])
    coefs = dot_full(inverse, total[:, :cols_dev])
    nrhs = rhs.shape[1]
    side_coeffs[...] = side[:, :nrhs]
    side_left[...] = rhs[...] - dot_full(panel[...], side)[:, :nrhs]
    updated[...] = front[...] - dot_full(panel[...], coefs)


def solution(mesh):
    n, ncols = mesh.shape["rows"], mesh.shape["cols"]

    def shards(parent_front, right_sides, child_values, block_owner, row_map, col_map):
        rows_dev, cols_dev = parent_front.shape
        child_rows, child_cols = child_values.shape
        nrhs = right_sides.shape[1]
        width = cols_dev + PANEL + -(-nrhs // LANES) * LANES
        levels = n.bit_length() - 1
        halving = min(levels, (PANEL // SUBLANES).bit_length() - 1)
        nparts = min(3, levels)
        tiles = width // LANES
        widest = max(tiles * (q + 1) // nparts - tiles * q // nparts for q in range(nparts)) * LANES
        landing_rows = sum((PANEL >> (t + 1)) if t < halving else SUBLANES for t in range(levels))
        block = child_rows // n
        vmem, anywhere = pl.BlockSpec(memory_space=pltpu.VMEM), pl.BlockSpec(memory_space=pl.ANY)
        return pl.pallas_call(
            functools.partial(kernel, n, ncols),
            out_shape=(
                jax.ShapeDtypeStruct((rows_dev, cols_dev), f32),
                jax.ShapeDtypeStruct((PANEL, nrhs), f32),
                jax.ShapeDtypeStruct((rows_dev, nrhs), f32),
            ),
            in_specs=[pl.BlockSpec(memory_space=pltpu.SMEM), anywhere, vmem, vmem, vmem, vmem],
            out_specs=(vmem, vmem, vmem),
            scratch_shapes=[
                pltpu.VMEM((rows_dev, cols_dev), f32),
                pltpu.VMEM((n, block, child_cols + LANES), f32),
                pltpu.VMEM((n, block, child_cols + LANES), f32),
                pltpu.VMEM((child_rows, child_cols + LANES), f32),
                pltpu.VMEM((cols_dev, child_cols), bf16),
                pltpu.VMEM((rows_dev, PANEL), f32),
                pltpu.VMEM((PANEL, width), f32),
                pltpu.VMEM((PANEL, width), f32),
                pltpu.VMEM((nparts, landing_rows, widest), f32),
                pltpu.SemaphoreType.DMA,
                pltpu.SemaphoreType.DMA((n,)),
                pltpu.SemaphoreType.DMA((n,)),
                pltpu.SemaphoreType.DMA((max(ncols - 1, 1),)),
                pltpu.SemaphoreType.DMA,
                pltpu.SemaphoreType.DMA((nparts, 2 * levels)),
                pltpu.SemaphoreType.DMA((nparts, 2 * levels)),
            ],
            compiler_params=pltpu.CompilerParams(collective_id=0, has_side_effects=True, vmem_limit_bytes=48 << 20),
        )(block_owner, parent_front, right_sides, child_values, row_map.reshape(1, -1), col_map.reshape(1, -1))

    in_specs = (
        P("rows", "cols"),
        P("rows", None),
        P("rows", "cols"),
        P("rows"),
        P("rows"),
        P("cols"),
    )
    out_specs = (P("rows", "cols"), P(), P("rows", None))
    return jax.shard_map(shards, mesh=mesh, in_specs=in_specs, out_specs=out_specs, check_vma=False)
```

```python
import functools

import jax
import jax.numpy as jnp
from jax import lax
from jax.experimental import pallas as pl
from jax.experimental.pallas import tpu as pltpu
from jax.sharding import PartitionSpec as P

PANEL = 128
LANES = 128
SUBLANES = 8
VMEM_LIMIT = 40 << 20
MESH = pl.DeviceIdType.MESH
f32 = jnp.float32
bf16 = jnp.bfloat16


def pieces(value):
    first = value.astype(bf16)
    rest = value - first.astype(f32)
    second = rest.astype(bf16)
    third = (rest - second.astype(f32)).astype(bf16)
    return first, second, third


def dot(left, right, dims, precision=None):
    return lax.dot_general(left, right, (dims, ((), ())), precision=precision, preferred_element_type=f32)


def dot_full(left, right, dims=((1,), (0,))):
    return dot(left, right, dims, lax.Precision.HIGHEST)


def sweep_pair(mat, k, lane, sub):
    row0, row1 = mat[k : k + 1, :], mat[k + 1 : k + 2, :]
    col0, col1 = mat[:, k : k + 1], mat[:, k + 1 : k + 2]
    a, b, d = mat[k : k + 1, k : k + 1], mat[k : k + 1, k + 1 : k + 2], mat[k + 1 : k + 2, k + 1 : k + 2]
    ia = 1.0 / a
    ratio = b * ia
    i11 = 1.0 / (d - b * ratio)
    i01 = -ratio * i11
    i00 = ia - ratio * i01
    top0, top1 = i00 * row0 + i01 * row1, i01 * row0 + i11 * row1
    side0, side1 = i00 * col0 + i01 * col1, i01 * col0 + i11 * col1
    lane_row = lane[:1]
    top0 = jnp.where(lane_row == k, -i00, jnp.where(lane_row == k + 1, -i01, top0))
    top1 = jnp.where(lane_row == k, -i01, jnp.where(lane_row == k + 1, -i11, top1))
    raw0 = i00 * row0 + i01 * row1
    raw1 = i01 * row0 + i11 * row1
    out = mat - col0 * raw0 - col1 * raw1
    out = jnp.where(lane == k, side0, jnp.where(lane == k + 1, side1, out))
    out = jnp.where(sub == k, top0, jnp.where(sub == k + 1, top1, out))
    return out


def sweep_groups(mat, count):
    size = mat.shape[0]
    lane = lax.broadcasted_iota(jnp.int32, mat.shape, 1)
    sub = lax.broadcasted_iota(jnp.int32, mat.shape, 0)

    def group(_, mat):
        for k in range(0, SUBLANES, 2):
            mat = sweep_pair(mat, k, lane, sub)
        mat = jnp.concatenate([mat[SUBLANES:], mat[:SUBLANES]], axis=0)
        return pltpu.roll(mat, size - SUBLANES, 1)

    return lax.fori_loop(0, count, group, mat)


def plan(n, width):
    levels = n.bit_length() - 1
    halving = min(levels, (PANEL // SUBLANES).bit_length() - 1)
    nparts = min(3, levels)
    tiles = width // LANES
    starts = [tiles * q // nparts * LANES for q in range(nparts + 1)]
    orders = [[(q + t) % nparts for t in range(nparts)] + list(range(nparts, levels)) for q in range(nparts)]
    single = max(halving - 2, 0)
    cuts = [(t, t + 1) for t in range(single)] + [(single, halving)]
    parts = [([order[a:b] for a, b in cuts], [[bit] for bit in order[halving:]]) for order in orders]
    return starts, parts, halving


def slots_of(n):
    levels = n.bit_length() - 1
    halving = min(levels, (PANEL // SUBLANES).bit_length() - 1)
    rows, count = 0, 0
    single = max(halving - 2, 0)
    size = PANEL
    for bits in [1] * single + [halving - single]:
        size >>= bits
        rows += ((1 << bits) - 1) * size
        count += (1 << bits) - 1
    rows += (levels - halving) * SUBLANES
    count += levels - halving
    return rows, count


def kernel(n, ncols, owner, parent, rhs_t, child_hbm, row_map, col_map, front, panel, coefs, side_t, left_t,
           child, send, recv, flat, hot, sides, prod, total, halves, gram, gram_in, gram_all,
           in_sem, a2a_send, a2a_recv, pan_send, pan_recv, gram_send, gram_recv, red_send, red_recv):
    row, col = lax.axis_index("rows"), lax.axis_index("cols")
    rows_dev, cols_dev = front.shape
    child_rows, child_cols = child.shape
    nrhs = rhs_t.shape[0]
    block = child_rows // n
    load_child = pltpu.make_async_copy(child_hbm, child, in_sem.at[0])
    load_child.start()
    load = pltpu.make_async_copy(parent, front, in_sem.at[1])
    load.start()

    barrier = pltpu.get_barrier_semaphore()
    for step in range(1, n):
        pl.semaphore_signal(barrier, inc=1, device_id=(lax.rem(row + step, n), col), device_id_type=MESH)
    for step in range(1, ncols):
        pl.semaphore_signal(barrier, inc=1, device_id=(row, lax.rem(col + step, ncols)), device_id_type=MESH)

    source = lax.broadcasted_iota(jnp.int32, (1, child_rows), 1)
    target = jnp.zeros((1, child_rows), jnp.int32)
    for k in range(n):
        target = jnp.where(source // block == k, owner[k] * block + source % block, target)
    place = lax.broadcasted_iota(jnp.int32, (child_rows, child_rows), 0) == target
    place_f = jnp.where(place, 1.0, 0.0).astype(f32)
    landing = jnp.sum(place_f * row_map[...].astype(f32), axis=1, keepdims=True)
    place_b = place_f.astype(bf16)
    load_child.wait()
    one, two, three = pieces(child[...])
    ordered = dot(place_b, one, ((1,), (0,))) + dot(place_b, two, ((1,), (0,))) + dot(place_b, three, ((1,), (0,)))
    landing = jnp.broadcast_to(landing, (child_rows, LANES))
    for k in range(n):
        send[k, :, :child_cols] = ordered[k * block : (k + 1) * block]
        send[k, :, child_cols:] = landing[k * block : (k + 1) * block]

    pl.semaphore_wait(barrier, n - 1 + ncols - 1)

    copies = []
    for step in range(1, n):
        peer = lax.rem(row + step, n)
        copy = pltpu.make_async_remote_copy(
            src_ref=send.at[peer], dst_ref=recv.at[row], send_sem=a2a_send.at[step], recv_sem=a2a_recv.at[step],
            device_id=(peer, col), device_id_type=MESH)
        copy.start()
        copies.append(copy)
    recv[row] = send[row]

    cols_at = lax.broadcasted_iota(jnp.int32, hot.shape, 0)
    hot[...] = jnp.where(cols_at == col_map[...], 1.0, 0.0).astype(f32).astype(bf16)
    padded = jnp.concatenate([rhs_t[...], jnp.zeros((sides.shape[1] - nrhs, rows_dev), f32)], axis=0)
    sides[...] = jnp.transpose(padded)
    load.wait()
    for copy in copies:
        copy.wait()

    for k in range(n):
        flat[k * block : (k + 1) * block, :] = recv[k]
    vals = jnp.concatenate(pieces(flat[:, :child_cols]), axis=0)
    where_rows = flat[:, child_cols:].astype(jnp.int32)
    rows_at = lax.broadcasted_iota(jnp.int32, where_rows.shape, 1)
    landed = jnp.concatenate(
        [jnp.where(where_rows == rows_at + t * LANES, 1.0, 0.0).astype(f32) for t in range(rows_dev // LANES)], axis=1)
    landed3 = jnp.concatenate([landed] * 3, axis=0).astype(bf16)

    def assemble(first, last):
        spread3 = dot(vals, hot[first:last, :], ((1,), (1,)))
        spread = spread3[:child_rows] + spread3[child_rows : 2 * child_rows] + spread3[2 * child_rows :]
        stacked = jnp.concatenate(pieces(spread), axis=0)
        front[:, first:last] = front[:, first:last] + dot(landed3, stacked, ((0,), (0,)))

    assemble(0, PANEL)
    pan_copies = [
        pltpu.make_async_remote_copy(
            src_ref=front.at[:, pl.ds(0, PANEL)], dst_ref=panel, send_sem=pan_send.at[step - 1], recv_sem=pan_recv,
            device_id=(row, step), device_id_type=MESH)
        for step in range(1, ncols)
    ]

    @pl.when(col == 0)
    def _():
        for copy in pan_copies:
            copy.start()
        panel[...] = front[:, :PANEL]

    assemble(PANEL, cols_dev)

    @pl.when(col == 0)
    def _():
        for copy in pan_copies:
            copy.wait_send()

    @pl.when(col != 0)
    def _():
        pan_copies[0].wait_recv()

    block_panel = panel[...]
    trans = ((0,), (0,))
    gram[...] = dot_full(block_panel, block_panel, trans)

    chunks = min(n, PANEL // SUBLANES)
    chunk = PANEL // chunks
    own_chunk = lax.rem(row, chunks)
    own_rows = pl.ds(pl.multiple_of(own_chunk * chunk, SUBLANES), chunk)
    gathers = []
    for step in range(1, n):
        peer = lax.rem(row + step, n)
        start = pl.multiple_of(lax.rem(peer, chunks) * chunk, SUBLANES)
        copy = pltpu.make_async_remote_copy(
            src_ref=gram.at[pl.ds(start, chunk)], dst_ref=gram_in.at[row],
            send_sem=gram_send.at[step], recv_sem=gram_recv.at[step], device_id=(peer, col), device_id_type=MESH)
        copy.start()
        gathers.append(copy)
    gram_in[row] = gram[own_rows, :]

    prod[:, :cols_dev] = dot_full(block_panel, front[...], trans)
    prod[:, cols_dev:] = dot_full(block_panel, sides[...], trans)

    starts, parts, halving = plan(n, prod.shape[1])
    base = [row * 0] * len(parts)
    nstages = len(parts[0][0])

    def own_bit(bit):
        return (row // (1 << bit)) % 2

    def members(bits):
        mine = sum(own_bit(bit) * (1 << i) for i, bit in enumerate(bits))
        others = []
        for d in range(1, 1 << len(bits)):
            code, peer = 0, row
            for i, bit in enumerate(bits):
                own = own_bit(bit)
                flip = d >> i & 1
                code = code + (1 - own if flip else own) * (1 << i)
                peer = peer + ((1 - 2 * own) * (1 << bit) if flip else 0)
            others.append((code, peer))
        return mine, others

    def send_stage(stage, at, slot, size, split):
        held = []
        for q, (groups, extras) in enumerate(parts):
            bits = groups[stage] if split else extras[stage]
            mine, others = members(bits)
            piece = size >> len(bits) if split else size
            keep = pl.multiple_of(base[q] + mine * piece if split else base[q], SUBLANES)
            width = starts[q + 1] - starts[q]
            sent = []
            for d, (code, peer) in enumerate(others):
                give = pl.multiple_of(base[q] + code * piece, SUBLANES) if split else keep
                copy = pltpu.make_async_remote_copy(
                    src_ref=prod.at[pl.ds(give, piece), pl.ds(starts[q], width)],
                    dst_ref=halves.at[q, pl.ds(at + d * piece, piece), pl.ds(0, width)],
                    send_sem=red_send.at[q, slot + d], recv_sem=red_recv.at[q, slot + d],
                    device_id=(peer, col), device_id_type=MESH)
                copy.start()
                sent.append((copy, at + d * piece))
            held.append((sent, keep, piece, width))
            base[q] = keep
        used = len(held[0][0])
        return held, at + used * held[0][2], slot + used, held[0][2]

    def add_stage(held):
        for q, (sent, keep, piece, width) in enumerate(held):
            for copy, _ in sent:
                copy.wait()
            spot = (pl.ds(keep, piece), slice(starts[q], starts[q + 1]))
            value = prod[spot]
            for _, at in sent:
                value = value + halves[q, at : at + piece, :width]
            prod[spot] = value

    def share_stage(stage, slot, piece):
        sent = []
        for q, (groups, _) in enumerate(parts):
            _, others = members(groups[stage])
            keep = pl.multiple_of(base[q], SUBLANES)
            spot = total.at[pl.ds(keep, piece), pl.ds(starts[q], starts[q + 1] - starts[q])]
            for d, (_, peer) in enumerate(others):
                copy = pltpu.make_async_remote_copy(
                    src_ref=spot, dst_ref=spot, send_sem=red_send.at[q, slot + d], recv_sem=red_recv.at[q, slot + d],
                    device_id=(peer, col), device_id_type=MESH)
                copy.start()
                sent.append(copy)
        return sent, slot + len(sent) // len(parts)

    marks = []
    at, slot, size = 0, 0, PANEL
    marks.append(list(base))
    held, at, slot, size = send_stage(0, at, slot, size, True)

    for copy in gathers:
        copy.wait()
    summed = gram_in[0]
    for k in range(1, n):
        summed = summed + gram_in[k]
    gram_all[own_rows, :] = summed
    spreads = []
    for step in range(1, chunks):
        peer = row - own_chunk + lax.rem(own_chunk + step, chunks)
        copy = pltpu.make_async_remote_copy(
            src_ref=gram_all.at[own_rows], dst_ref=gram_all.at[own_rows],
            send_sem=gram_send.at[n + step], recv_sem=gram_recv.at[n + step],
            device_id=(peer, col), device_id_type=MESH)
        copy.start()
        spreads.append(copy)

    for stage in range(1, nstages):
        add_stage(held)
        marks.append(list(base))
        held, at, slot, size = send_stage(stage, at, slot, size, True)
    for copy in spreads:
        copy.wait()
    turns = PANEL // SUBLANES
    mat, done = gram_all[...], 0

    def turn_by(mat, done, share):
        upto = min(turns, done + share)
        return (sweep_groups(mat, upto - done) if upto > done else mat), upto

    mat, done = turn_by(mat, done, 3)
    add_stage(held)
    for stage in range(len(parts[0][1])):
        held, at, slot, size = send_stage(stage, at, slot, size, False)
        add_stage(held)
    for q in range(len(parts)):
        spot = (pl.ds(pl.multiple_of(base[q], SUBLANES), size), slice(starts[q], starts[q + 1]))
        total[spot] = prod[spot]
    for stage in reversed(range(nstages)):
        sent, slot = share_stage(stage, slot, size)
        mat, done = turn_by(mat, done, turns if stage == 0 else 4)
        for copy in sent:
            copy.wait()
        size <<= len(parts[0][0][stage])
        for q in range(len(parts)):
            base[q] = marks[stage][q]

    inverse = -mat
    side = dot_full(inverse, total[:, cols_dev:])
    coefs[...] = dot_full(inverse, total[:, :cols_dev])
    side_t[...] = jnp.transpose(side)[:nrhs]
    left_t[...] = rhs_t[...] - jnp.transpose(dot_full(panel[...], side))[:nrhs]


def solution(mesh):
    n, ncols = mesh.shape["rows"], mesh.shape["cols"]

    def shards(parent_front, right_sides, child_values, block_owner, row_map, col_map):
        rows_dev, cols_dev = parent_front.shape
        child_rows, child_cols = child_values.shape
        nrhs = right_sides.shape[1]
        side_width = -(-nrhs // LANES) * LANES
        width = cols_dev + side_width
        starts, parts, _ = plan(n, width)
        nparts = len(parts)
        widest = max(starts[q + 1] - starts[q] for q in range(nparts))
        landing_rows, slots = slots_of(n)
        block = child_rows // n
        chunks = min(n, PANEL // SUBLANES)
        vmem, anywhere = pl.BlockSpec(memory_space=pltpu.VMEM), pl.BlockSpec(memory_space=pl.ANY)
        dma = pltpu.SemaphoreType.DMA
        front, panel, coefs, side_t, left_t = pl.pallas_call(
            functools.partial(kernel, n, ncols),
            out_shape=(
                jax.ShapeDtypeStruct((rows_dev, cols_dev), f32),
                jax.ShapeDtypeStruct((rows_dev, PANEL), f32),
                jax.ShapeDtypeStruct((PANEL, cols_dev), f32),
                jax.ShapeDtypeStruct((nrhs, PANEL), f32),
                jax.ShapeDtypeStruct((nrhs, rows_dev), f32),
            ),
            in_specs=[pl.BlockSpec(memory_space=pltpu.SMEM), anywhere, vmem, anywhere, vmem, vmem],
            out_specs=(vmem, vmem, vmem, vmem, vmem),
            scratch_shapes=[
                pltpu.VMEM((child_rows, child_cols), f32),
                pltpu.VMEM((n, block, child_cols + LANES), f32),
                pltpu.VMEM((n, block, child_cols + LANES), f32),
                pltpu.VMEM((child_rows, child_cols + LANES), f32),
                pltpu.VMEM((cols_dev, child_cols), bf16),
                pltpu.VMEM((rows_dev, side_width), f32),
                pltpu.VMEM((PANEL, width), f32),
                pltpu.VMEM((PANEL, width), f32),
                pltpu.VMEM((nparts, landing_rows, widest), f32),
                pltpu.VMEM((PANEL, PANEL), f32),
                pltpu.VMEM((n, PANEL // chunks, PANEL), f32),
                pltpu.VMEM((PANEL, PANEL), f32),
                dma((2,)),
                dma((n,)),
                dma((n,)),
                dma((max(ncols - 1, 1),)),
                dma,
                dma((n + chunks,)),
                dma((n + chunks,)),
                dma((nparts, 2 * slots)),
                dma((nparts, 2 * slots)),
            ],
            compiler_params=pltpu.CompilerParams(collective_id=0, has_side_effects=True, vmem_limit_bytes=VMEM_LIMIT),
        )(block_owner, parent_front, right_sides.T, child_values, row_map.reshape(1, -1), col_map.reshape(1, -1))
        updated = front - jnp.dot(panel, coefs, precision=lax.Precision.HIGHEST, preferred_element_type=f32)
        return updated, side_t.T, left_t.T

    in_specs = (
        P("rows", "cols"),
        P("rows", None),
        P("rows", "cols"),
        P("rows"),
        P("rows"),
        P("cols"),
    )
    out_specs = (P("rows", "cols"), P(), P("rows", None))
    return jax.shard_map(shards, mesh=mesh, in_specs=in_specs, out_specs=out_specs, check_vma=False)
```

```python
import functools

import jax
import jax.numpy as jnp
from jax import lax
from jax.experimental import pallas as pl
from jax.experimental.pallas import tpu as pltpu
from jax.sharding import PartitionSpec as P

PANEL = 128
LANES = 128
SUBLANES = 8
TILE = 256
VMEM_LIMIT = 40 << 20
MESH = pl.DeviceIdType.MESH
f32 = jnp.float32
bf16 = jnp.bfloat16


def pieces(value):
    first = value.astype(bf16)
    rest = value - first.astype(f32)
    second = rest.astype(bf16)
    third = (rest - second.astype(f32)).astype(bf16)
    return first, second, third


def dot(left, right, dims, precision=None):
    return lax.dot_general(left, right, (dims, ((), ())), precision=precision, preferred_element_type=f32)


def dot_full(left, right, dims=((1,), (0,))):
    return dot(left, right, dims, lax.Precision.HIGHEST)


def inverse_pair(a, b, d):
    ia = 1.0 / a
    ratio = b * ia
    i11 = 1.0 / (d - b * ratio)
    i01 = -ratio * i11
    return ia - ratio * i01, i01, i11


def sweep_four(mat, k, lane):
    cols = [mat[:, k + j : k + j + 1] for j in range(4)]
    rows = [mat[k + j : k + j + 1, :] for j in range(4)]
    d = [[jnp.broadcast_to(mat[k + i : k + i + 1, k + j : k + j + 1], (1, mat.shape[1])) for j in range(i + 1)] for i in range(4)]
    a00, a01, a11 = inverse_pair(d[0][0], d[1][0], d[1][1])
    l20, l21 = d[2][0] * a00 + d[2][1] * a01, d[2][0] * a01 + d[2][1] * a11
    l30, l31 = d[3][0] * a00 + d[3][1] * a01, d[3][0] * a01 + d[3][1] * a11
    s22 = d[2][2] - (l20 * d[2][0] + l21 * d[2][1])
    s32 = d[3][2] - (l30 * d[2][0] + l31 * d[2][1])
    s33 = d[3][3] - (l30 * d[3][0] + l31 * d[3][1])
    e22, e32, e33 = inverse_pair(s22, s32, s33)
    e20, e21 = -(e22 * l20 + e32 * l30), -(e22 * l21 + e32 * l31)
    e30, e31 = -(e32 * l20 + e33 * l30), -(e32 * l21 + e33 * l31)
    e00 = a00 - (l20 * e20 + l30 * e30)
    e10 = a01 - (l21 * e20 + l31 * e30)
    e11 = a11 - (l21 * e21 + l31 * e31)
    e = [[e00, e10, e20, e30], [e10, e11, e21, e31], [e20, e21, e22, e32], [e30, e31, e32, e33]]
    lane_row = lane[:1]
    tops = []
    for i in range(4):
        top = (e[i][0] * rows[0] + e[i][1] * rows[1]) + (e[i][2] * rows[2] + e[i][3] * rows[3])
        for j in range(4):
            top = jnp.where(lane_row == k + j, -e[i][j], top)
        tops.append(top)
    out = jnp.where((lane >= k) & (lane < k + 4), 0.0, mat)
    out = out - ((cols[0] * tops[0] + cols[1] * tops[1]) + (cols[2] * tops[2] + cols[3] * tops[3]))
    head = out[:SUBLANES]
    sub = lax.broadcasted_iota(jnp.int32, head.shape, 0)
    for j in range(4):
        head = jnp.where(sub == k + j, tops[j], head)
    return jnp.concatenate([head, out[SUBLANES:]], axis=0)


def sweep_groups(mat, count):
    size = mat.shape[0]
    lane = lax.broadcasted_iota(jnp.int32, mat.shape, 1)

    def group(_, mat):
        for k in range(0, SUBLANES, 4):
            mat = sweep_four(mat, k, lane)
        mat = jnp.concatenate([mat[SUBLANES:], mat[:SUBLANES]], axis=0)
        return pltpu.roll(mat, size - SUBLANES, 1)

    return lax.fori_loop(0, count, group, mat)


def plan(n, width):
    levels = n.bit_length() - 1
    halving = min(levels, (PANEL // SUBLANES).bit_length() - 1)
    nparts = min(3, levels)
    tiles = width // LANES
    starts = [tiles * q // nparts * LANES for q in range(nparts + 1)]
    orders = [[(q + t) % nparts for t in range(nparts)] + list(range(nparts, levels)) for q in range(nparts)]
    single = max(halving - 2, 0)
    cuts = [(t, t + 1) for t in range(single)] + [(single, halving)]
    parts = [([order[a:b] for a, b in cuts], [[bit] for bit in order[halving:]]) for order in orders]
    return starts, parts, halving


def slots_of(n):
    levels = n.bit_length() - 1
    halving = min(levels, (PANEL // SUBLANES).bit_length() - 1)
    rows, count = 0, 0
    single = max(halving - 2, 0)
    size = PANEL
    for bits in [1] * single + [halving - single]:
        size >>= bits
        rows += ((1 << bits) - 1) * size
        count += (1 << bits) - 1
    rows += (levels - halving) * SUBLANES
    count += levels - halving
    return rows, count


def kernel(n, ncols, owner_hbm, parent, rhs_hbm, child_hbm, row_map_hbm, col_map_hbm, front, panel, coefs, side_out,
           owner, rhs_t, row_map, col_map, child, send, recv, flat, hot, sides, prod, total, halves, gram, gram_in, gram_all,
           in_sem, a2a_send, a2a_recv, pan_send, pan_recv, gram_send, gram_recv, red_send, red_recv):
    row, col = lax.axis_index("rows"), lax.axis_index("cols")
    rows_dev, cols_dev = front.shape
    child_rows, child_cols = child.shape
    nrhs = rhs_t.shape[0]
    block = child_rows // n
    first_loads = [
        pltpu.make_async_copy(source, target, in_sem.at[k])
        for k, (source, target) in enumerate([(owner_hbm, owner), (row_map_hbm, row_map), (child_hbm, child)])
    ]
    later_loads = [
        pltpu.make_async_copy(source, target, in_sem.at[3 + k])
        for k, (source, target) in enumerate([(col_map_hbm, col_map), (rhs_hbm, rhs_t), (parent, front)])
    ]
    for load in first_loads + later_loads:
        load.start()

    barrier = pltpu.get_barrier_semaphore()
    for step in range(1, n):
        pl.semaphore_signal(barrier, inc=1, device_id=(lax.rem(row + step, n), col), device_id_type=MESH)
    for step in range(1, ncols):
        pl.semaphore_signal(barrier, inc=1, device_id=(row, lax.rem(col + step, ncols)), device_id_type=MESH)

    for load in first_loads:
        load.wait()
    source = lax.broadcasted_iota(jnp.int32, (1, child_rows), 1)
    target = jnp.zeros((1, child_rows), jnp.int32)
    for k in range(n):
        target = jnp.where(source // block == k, owner[k] * block + source % block, target)
    place = lax.broadcasted_iota(jnp.int32, (child_rows, child_rows), 0) == target
    place_f = jnp.where(place, 1.0, 0.0).astype(f32)
    landing = jnp.sum(place_f * row_map[...].astype(f32), axis=1, keepdims=True)
    place_b = place_f.astype(bf16)
    one, two, three = pieces(child[...])
    ordered = dot(place_b, one, ((1,), (0,))) + dot(place_b, two, ((1,), (0,))) + dot(place_b, three, ((1,), (0,)))
    landing = jnp.broadcast_to(landing, (child_rows, LANES))
    for k in range(n):
        send[k, :, :child_cols] = ordered[k * block : (k + 1) * block]
        send[k, :, child_cols:] = landing[k * block : (k + 1) * block]

    pl.semaphore_wait(barrier, n - 1 + ncols - 1)

    copies = []
    for step in range(1, n):
        peer = lax.rem(row + step, n)
        copy = pltpu.make_async_remote_copy(
            src_ref=send.at[peer], dst_ref=recv.at[row], send_sem=a2a_send.at[step], recv_sem=a2a_recv.at[step],
            device_id=(peer, col), device_id_type=MESH)
        copy.start()
        copies.append(copy)
    recv[row] = send[row]

    for load in later_loads:
        load.wait()
    cols_at = lax.broadcasted_iota(jnp.int32, hot.shape, 0)
    hot[...] = jnp.where(cols_at == col_map[...], 1.0, 0.0).astype(f32).astype(bf16)
    padded = jnp.concatenate([rhs_t[...], jnp.zeros((sides.shape[1] - nrhs, rows_dev), f32)], axis=0)
    sides[...] = jnp.transpose(padded)
    for copy in copies:
        copy.wait()

    for k in range(n):
        flat[k * block : (k + 1) * block, :] = recv[k]
    vals = jnp.concatenate(pieces(flat[:, :child_cols]), axis=0)
    where_rows = flat[:, child_cols:].astype(jnp.int32)
    rows_at = lax.broadcasted_iota(jnp.int32, where_rows.shape, 1)
    landed = jnp.concatenate(
        [jnp.where(where_rows == rows_at + t * LANES, 1.0, 0.0).astype(f32) for t in range(rows_dev // LANES)], axis=1)
    landed3 = jnp.concatenate([landed] * 3, axis=0).astype(bf16)

    def assemble(first, last):
        spread3 = dot(vals, hot[first:last, :], ((1,), (1,)))
        spread = spread3[:child_rows] + spread3[child_rows : 2 * child_rows] + spread3[2 * child_rows :]
        stacked = jnp.concatenate(pieces(spread), axis=0)
        front[:, first:last] = front[:, first:last] + dot(landed3, stacked, ((0,), (0,)))

    assemble(0, PANEL)
    pan_copies = [
        pltpu.make_async_remote_copy(
            src_ref=front.at[:, pl.ds(0, PANEL)], dst_ref=panel, send_sem=pan_send.at[step - 1], recv_sem=pan_recv,
            device_id=(row, step), device_id_type=MESH)
        for step in range(1, ncols)
    ]

    @pl.when(col == 0)
    def _():
        for copy in pan_copies:
            copy.start()
        panel[...] = front[:, :PANEL]

    assemble(PANEL, cols_dev)

    @pl.when(col == 0)
    def _():
        for copy in pan_copies:
            copy.wait_send()

    @pl.when(col != 0)
    def _():
        pan_copies[0].wait_recv()

    block_panel = panel[...]
    trans = ((0,), (0,))
    gram[...] = dot_full(block_panel, block_panel, trans)

    chunks = min(n, PANEL // SUBLANES)
    chunk = PANEL // chunks
    own_chunk = lax.rem(row, chunks)
    own_rows = pl.ds(pl.multiple_of(own_chunk * chunk, SUBLANES), chunk)
    gathers = []
    for step in range(1, n):
        peer = lax.rem(row + step, n)
        start = pl.multiple_of(lax.rem(peer, chunks) * chunk, SUBLANES)
        copy = pltpu.make_async_remote_copy(
            src_ref=gram.at[pl.ds(start, chunk)], dst_ref=gram_in.at[row],
            send_sem=gram_send.at[step], recv_sem=gram_recv.at[step], device_id=(peer, col), device_id_type=MESH)
        copy.start()
        gathers.append(copy)
    gram_in[row] = gram[own_rows, :]

    prod[:, :cols_dev] = dot_full(block_panel, front[...], trans)
    prod[:, cols_dev:] = dot_full(block_panel, sides[...], trans)

    starts, parts, halving = plan(n, prod.shape[1])
    base = [row * 0] * len(parts)
    nstages = len(parts[0][0])

    def own_bit(bit):
        return (row // (1 << bit)) % 2

    def members(bits):
        mine = sum(own_bit(bit) * (1 << i) for i, bit in enumerate(bits))
        others = []
        for d in range(1, 1 << len(bits)):
            code, peer = 0, row
            for i, bit in enumerate(bits):
                own = own_bit(bit)
                flip = d >> i & 1
                code = code + (1 - own if flip else own) * (1 << i)
                peer = peer + ((1 - 2 * own) * (1 << bit) if flip else 0)
            others.append((code, peer))
        return mine, others

    def send_stage(stage, at, slot, size, split):
        held = []
        for q, (groups, extras) in enumerate(parts):
            bits = groups[stage] if split else extras[stage]
            mine, others = members(bits)
            piece = size >> len(bits) if split else size
            keep = pl.multiple_of(base[q] + mine * piece if split else base[q], SUBLANES)
            width = starts[q + 1] - starts[q]
            sent = []
            for d, (code, peer) in enumerate(others):
                give = pl.multiple_of(base[q] + code * piece, SUBLANES) if split else keep
                copy = pltpu.make_async_remote_copy(
                    src_ref=prod.at[pl.ds(give, piece), pl.ds(starts[q], width)],
                    dst_ref=halves.at[q, pl.ds(at + d * piece, piece), pl.ds(0, width)],
                    send_sem=red_send.at[q, slot + d], recv_sem=red_recv.at[q, slot + d],
                    device_id=(peer, col), device_id_type=MESH)
                copy.start()
                sent.append((copy, at + d * piece))
            held.append((sent, keep, piece, width))
            base[q] = keep
        used = len(held[0][0])
        return held, at + used * held[0][2], slot + used, held[0][2]

    def add_stage(held):
        for q, (sent, keep, piece, width) in enumerate(held):
            for copy, _ in sent:
                copy.wait()
            spot = (pl.ds(keep, piece), slice(starts[q], starts[q + 1]))
            value = prod[spot]
            for _, at in sent:
                value = value + halves[q, at : at + piece, :width]
            prod[spot] = value

    def share_stage(stage, slot, piece):
        sent = []
        for q, (groups, _) in enumerate(parts):
            _, others = members(groups[stage])
            keep = pl.multiple_of(base[q], SUBLANES)
            spot = total.at[pl.ds(keep, piece), pl.ds(starts[q], starts[q + 1] - starts[q])]
            for d, (_, peer) in enumerate(others):
                copy = pltpu.make_async_remote_copy(
                    src_ref=spot, dst_ref=spot, send_sem=red_send.at[q, slot + d], recv_sem=red_recv.at[q, slot + d],
                    device_id=(peer, col), device_id_type=MESH)
                copy.start()
                sent.append(copy)
        return sent, slot + len(sent) // len(parts)

    marks = []
    at, slot, size = 0, 0, PANEL
    marks.append(list(base))
    held, at, slot, size = send_stage(0, at, slot, size, True)

    for copy in gathers:
        copy.wait()
    summed = gram_in[0]
    for k in range(1, n):
        summed = summed + gram_in[k]
    gram_all[own_rows, :] = summed
    spreads = []
    for step in range(1, chunks):
        peer = row - own_chunk + lax.rem(own_chunk + step, chunks)
        copy = pltpu.make_async_remote_copy(
            src_ref=gram_all.at[own_rows], dst_ref=gram_all.at[own_rows],
            send_sem=gram_send.at[n + step], recv_sem=gram_recv.at[n + step],
            device_id=(peer, col), device_id_type=MESH)
        copy.start()
        spreads.append(copy)

    for stage in range(1, nstages):
        add_stage(held)
        marks.append(list(base))
        held, at, slot, size = send_stage(stage, at, slot, size, True)
    for copy in spreads:
        copy.wait()
    turns = PANEL // SUBLANES
    mat, done = gram_all[...], 0

    def turn_by(mat, done, share):
        upto = min(turns, done + share)
        return (sweep_groups(mat, upto - done) if upto > done else mat), upto

    mat, done = turn_by(mat, done, 3)
    add_stage(held)
    for stage in range(len(parts[0][1])):
        held, at, slot, size = send_stage(stage, at, slot, size, False)
        add_stage(held)
    for q in range(len(parts)):
        spot = (pl.ds(pl.multiple_of(base[q], SUBLANES), size), slice(starts[q], starts[q + 1]))
        total[spot] = prod[spot]
    for stage in reversed(range(nstages)):
        sent, slot = share_stage(stage, slot, size)
        mat, done = turn_by(mat, done, turns if stage == 0 else 4)
        for copy in sent:
            copy.wait()
        size <<= len(parts[0][0][stage])
        for q in range(len(parts)):
            base[q] = marks[stage][q]

    inverse = -mat
    side_out[...] = dot_full(inverse, total[:, cols_dev:])
    coefs[...] = dot_full(inverse, total[:, :cols_dev])


def finish(front, panel, coefs, side, rhs_t, updated, side_t, left_t, stage, sems):
    nrhs = rhs_t.shape[0]
    tile = stage.shape[2]
    high, low, _ = pieces(panel[...])
    left = jnp.concatenate([high, high, low], axis=1)

    def product(right):
        top, rest, _ = pieces(right)
        return dot(left, jnp.concatenate([top, rest, top], axis=0), ((1,), (0,)))

    copies = []
    for t in range(stage.shape[0]):
        at = slice(t * tile, (t + 1) * tile)
        stage[t] = front[:, at] - product(coefs[:, at])
        copy = pltpu.make_async_copy(stage.at[t], updated.at[:, pl.ds(t * tile, tile)], sems.at[t])
        copy.start()
        copies.append(copy)
    sides = side[...]
    side_t[...] = jnp.transpose(sides)[:nrhs]
    left_t[...] = rhs_t[...] - jnp.transpose(product(sides))[:nrhs]
    for copy in copies:
        copy.wait()


def solution(mesh):
    n, ncols = mesh.shape["rows"], mesh.shape["cols"]

    def shards(parent_front, right_sides, child_values, block_owner, row_map, col_map):
        rows_dev, cols_dev = parent_front.shape
        child_rows, child_cols = child_values.shape
        nrhs = right_sides.shape[1]
        side_width = -(-nrhs // LANES) * LANES
        width = cols_dev + side_width
        starts, parts, _ = plan(n, width)
        nparts = len(parts)
        widest = max(starts[q + 1] - starts[q] for q in range(nparts))
        landing_rows, slots = slots_of(n)
        block = child_rows // n
        chunks = min(n, PANEL // SUBLANES)
        vmem = pl.BlockSpec(memory_space=pltpu.VMEM)
        dma = pltpu.SemaphoreType.DMA
        hbm = pl.BlockSpec(memory_space=pltpu.HBM)
        rhs_t = right_sides.T
        front, panel, coefs, side = pl.pallas_call(
            functools.partial(kernel, n, ncols),
            out_shape=(
                jax.ShapeDtypeStruct((rows_dev, cols_dev), f32),
                jax.ShapeDtypeStruct((rows_dev, PANEL), f32),
                jax.ShapeDtypeStruct((PANEL, cols_dev), f32),
                jax.ShapeDtypeStruct((PANEL, side_width), f32),
            ),
            in_specs=[hbm] * 6,
            out_specs=(vmem, vmem, vmem, vmem),
            scratch_shapes=[
                pltpu.SMEM(block_owner.shape, jnp.int32),
                pltpu.VMEM((nrhs, rows_dev), f32),
                pltpu.VMEM((1, child_rows), jnp.int32),
                pltpu.VMEM((1, child_cols), jnp.int32),
                pltpu.VMEM((child_rows, child_cols), f32),
                pltpu.VMEM((n, block, child_cols + LANES), f32),
                pltpu.VMEM((n, block, child_cols + LANES), f32),
                pltpu.VMEM((child_rows, child_cols + LANES), f32),
                pltpu.VMEM((cols_dev, child_cols), bf16),
                pltpu.VMEM((rows_dev, side_width), f32),
                pltpu.VMEM((PANEL, width), f32),
                pltpu.VMEM((PANEL, width), f32),
                pltpu.VMEM((nparts, landing_rows, widest), f32),
                pltpu.VMEM((PANEL, PANEL), f32),
                pltpu.VMEM((n, PANEL // chunks, PANEL), f32),
                pltpu.VMEM((PANEL, PANEL), f32),
                dma((6,)),
                dma((n,)),
                dma((n,)),
                dma((max(ncols - 1, 1),)),
                dma,
                dma((n + chunks,)),
                dma((n + chunks,)),
                dma((nparts, 2 * slots)),
                dma((nparts, 2 * slots)),
            ],
            compiler_params=pltpu.CompilerParams(collective_id=0, has_side_effects=True, vmem_limit_bytes=VMEM_LIMIT),
        )(block_owner, parent_front, rhs_t, child_values, row_map.reshape(1, -1), col_map.reshape(1, -1))
        tile = min(TILE, cols_dev)
        updated, side_t, left_t = pl.pallas_call(
            finish,
            out_shape=(
                jax.ShapeDtypeStruct((rows_dev, cols_dev), f32),
                jax.ShapeDtypeStruct((nrhs, PANEL), f32),
                jax.ShapeDtypeStruct((nrhs, rows_dev), f32),
            ),
            in_specs=[vmem] * 5,
            out_specs=(hbm, vmem, vmem),
            scratch_shapes=[pltpu.VMEM((cols_dev // tile, rows_dev, tile), f32), dma((cols_dev // tile,))],
            compiler_params=pltpu.CompilerParams(vmem_limit_bytes=16 << 20),
        )(front, panel, coefs, side, rhs_t)
        return updated, side_t.T, left_t.T

    in_specs = (
        P("rows", "cols"),
        P("rows", None),
        P("rows", "cols"),
        P("rows"),
        P("rows"),
        P("cols"),
    )
    out_specs = (P("rows", "cols"), P(), P("rows", None))
    return jax.shard_map(shards, mesh=mesh, in_specs=in_specs, out_specs=out_specs, check_vma=False)
```

```python
import functools

import jax
import jax.numpy as jnp
from jax import lax
from jax.experimental import pallas as pl
from jax.experimental.pallas import tpu as pltpu
from jax.sharding import PartitionSpec as P

PANEL = 128
LANES = 128
SUBLANES = 8
TILE = 256
VMEM_LIMIT = 67043328
MESH = pl.DeviceIdType.MESH
f32 = jnp.float32
bf16 = jnp.bfloat16


def pieces(value):
    first = value.astype(bf16)
    rest = value - first.astype(f32)
    second = rest.astype(bf16)
    third = (rest - second.astype(f32)).astype(bf16)
    return first, second, third


def dot(left, right, dims, precision=None):
    return lax.dot_general(left, right, (dims, ((), ())), precision=precision, preferred_element_type=f32)


def dot_full(left, right, dims=((1,), (0,))):
    return dot(left, right, dims, lax.Precision.HIGHEST)


def inverse_pair(a, b, d):
    ia = 1.0 / a
    ratio = b * ia
    i11 = 1.0 / (d - b * ratio)
    i01 = -ratio * i11
    return ia - ratio * i01, i01, i11


def sweep_four(mat, k, lane):
    cols = [mat[:, k + j : k + j + 1] for j in range(4)]
    rows = [mat[k + j : k + j + 1, :] for j in range(4)]
    d = [[jnp.broadcast_to(mat[k + i : k + i + 1, k + j : k + j + 1], (1, mat.shape[1])) for j in range(i + 1)] for i in range(4)]
    a00, a01, a11 = inverse_pair(d[0][0], d[1][0], d[1][1])
    l20, l21 = d[2][0] * a00 + d[2][1] * a01, d[2][0] * a01 + d[2][1] * a11
    l30, l31 = d[3][0] * a00 + d[3][1] * a01, d[3][0] * a01 + d[3][1] * a11
    s22 = d[2][2] - (l20 * d[2][0] + l21 * d[2][1])
    s32 = d[3][2] - (l30 * d[2][0] + l31 * d[2][1])
    s33 = d[3][3] - (l30 * d[3][0] + l31 * d[3][1])
    e22, e32, e33 = inverse_pair(s22, s32, s33)
    e20, e21 = -(e22 * l20 + e32 * l30), -(e22 * l21 + e32 * l31)
    e30, e31 = -(e32 * l20 + e33 * l30), -(e32 * l21 + e33 * l31)
    e00 = a00 - (l20 * e20 + l30 * e30)
    e10 = a01 - (l21 * e20 + l31 * e30)
    e11 = a11 - (l21 * e21 + l31 * e31)
    e = [[e00, e10, e20, e30], [e10, e11, e21, e31], [e20, e21, e22, e32], [e30, e31, e32, e33]]
    lane_row = lane[:1]
    tops = []
    for i in range(4):
        top = (e[i][0] * rows[0] + e[i][1] * rows[1]) + (e[i][2] * rows[2] + e[i][3] * rows[3])
        for j in range(4):
            top = jnp.where(lane_row == k + j, -e[i][j], top)
        tops.append(top)
    out = jnp.where((lane >= k) & (lane < k + 4), 0.0, mat)
    out = out - ((cols[0] * tops[0] + cols[1] * tops[1]) + (cols[2] * tops[2] + cols[3] * tops[3]))
    head = out[:SUBLANES]
    sub = lax.broadcasted_iota(jnp.int32, head.shape, 0)
    for j in range(4):
        head = jnp.where(sub == k + j, tops[j], head)
    return jnp.concatenate([head, out[SUBLANES:]], axis=0)


def sweep_groups(mat, count):
    size = mat.shape[0]
    lane = lax.broadcasted_iota(jnp.int32, mat.shape, 1)

    def group(_, mat):
        for k in range(0, SUBLANES, 4):
            mat = sweep_four(mat, k, lane)
        mat = jnp.concatenate([mat[SUBLANES:], mat[:SUBLANES]], axis=0)
        return pltpu.roll(mat, size - SUBLANES, 1)

    return lax.fori_loop(0, count, group, mat)


def plan(n, width):
    levels = n.bit_length() - 1
    halving = min(levels, (PANEL // SUBLANES).bit_length() - 1)
    nparts = min(3, levels)
    tiles = width // LANES
    starts = [tiles * q // nparts * LANES for q in range(nparts + 1)]
    orders = [[(q + t) % nparts for t in range(nparts)] + list(range(nparts, levels)) for q in range(nparts)]
    single = max(halving - 2, 0)
    cuts = [(t, t + 1) for t in range(single)] + [(single, halving)]
    parts = [([order[a:b] for a, b in cuts], [[bit] for bit in order[halving:]]) for order in orders]
    return starts, parts, halving


def slots_of(n):
    levels = n.bit_length() - 1
    halving = min(levels, (PANEL // SUBLANES).bit_length() - 1)
    rows, count = 0, 0
    single = max(halving - 2, 0)
    size = PANEL
    for bits in [1] * single + [halving - single]:
        size >>= bits
        rows += ((1 << bits) - 1) * size
        count += (1 << bits) - 1
    rows += (levels - halving) * SUBLANES
    count += levels - halving
    return rows, count


def kernel(n, ncols, owner_hbm, parent, rhs_hbm, child_hbm, row_map_hbm, col_map_hbm,
           front_out, panel_out, coefs_out, side_out, front, panel, coefs, side, out_sem, owner, rhs_t, row_map, col_map, child, send, recv, flat, hot, sides, prod, total, halves, gram, gram_in, gram_all,
           in_sem, a2a_send, a2a_recv, pan_send, pan_recv, gram_send, gram_recv, red_send, red_recv):
    row, col = lax.axis_index("rows"), lax.axis_index("cols")
    rows_dev, cols_dev = front.shape
    child_rows, child_cols = child.shape
    nrhs = rhs_t.shape[0]
    block = child_rows // n
    first_loads = [
        pltpu.make_async_copy(source, target, in_sem.at[k])
        for k, (source, target) in enumerate([(owner_hbm, owner), (row_map_hbm, row_map), (child_hbm, child)])
    ]
    later_loads = [
        pltpu.make_async_copy(source, target, in_sem.at[3 + k])
        for k, (source, target) in enumerate([(col_map_hbm, col_map), (rhs_hbm, rhs_t), (parent, front)])
    ]
    for load in first_loads + later_loads:
        load.start()

    barrier = pltpu.get_barrier_semaphore()
    for step in range(1, n):
        pl.semaphore_signal(barrier, inc=1, device_id=(lax.rem(row + step, n), col), device_id_type=MESH)
    for step in range(1, ncols):
        pl.semaphore_signal(barrier, inc=1, device_id=(row, lax.rem(col + step, ncols)), device_id_type=MESH)

    for load in first_loads:
        load.wait()
    source = lax.broadcasted_iota(jnp.int32, (1, child_rows), 1)
    target = jnp.zeros((1, child_rows), jnp.int32)
    for k in range(n):
        target = jnp.where(source // block == k, owner[k] * block + source % block, target)
    place = lax.broadcasted_iota(jnp.int32, (child_rows, child_rows), 0) == target
    place_f = jnp.where(place, 1.0, 0.0).astype(f32)
    landing = jnp.sum(place_f * row_map[...].astype(f32), axis=1, keepdims=True)
    place_b = place_f.astype(bf16)
    one, two, three = pieces(child[...])
    ordered = dot(place_b, one, ((1,), (0,))) + dot(place_b, two, ((1,), (0,))) + dot(place_b, three, ((1,), (0,)))
    landing = jnp.broadcast_to(landing, (child_rows, LANES))
    for k in range(n):
        send[k, :, :child_cols] = ordered[k * block : (k + 1) * block]
        send[k, :, child_cols:] = landing[k * block : (k + 1) * block]

    pl.semaphore_wait(barrier, n - 1 + ncols - 1)

    copies = []
    for step in range(1, n):
        peer = lax.rem(row + step, n)
        copy = pltpu.make_async_remote_copy(
            src_ref=send.at[peer], dst_ref=recv.at[row], send_sem=a2a_send.at[step], recv_sem=a2a_recv.at[step],
            device_id=(peer, col), device_id_type=MESH)
        copy.start()
        copies.append(copy)
    recv[row] = send[row]

    for load in later_loads:
        load.wait()
    cols_at = lax.broadcasted_iota(jnp.int32, hot.shape, 0)
    hot[...] = jnp.where(cols_at == col_map[...], 1.0, 0.0).astype(f32).astype(bf16)
    padded = jnp.concatenate([rhs_t[...], jnp.zeros((sides.shape[1] - nrhs, rows_dev), f32)], axis=0)
    sides[...] = jnp.transpose(padded)
    for copy in copies:
        copy.wait()

    for k in range(n):
        flat[k * block : (k + 1) * block, :] = recv[k]
    vals = jnp.concatenate(pieces(flat[:, :child_cols]), axis=0)
    where_rows = flat[:, child_cols:].astype(jnp.int32)
    rows_at = lax.broadcasted_iota(jnp.int32, where_rows.shape, 1)
    landed = jnp.concatenate(
        [jnp.where(where_rows == rows_at + t * LANES, 1.0, 0.0).astype(f32) for t in range(rows_dev // LANES)], axis=1)
    landed3 = jnp.concatenate([landed] * 3, axis=0).astype(bf16)

    def assemble(first, last):
        spread3 = dot(vals, hot[first:last, :], ((1,), (1,)))
        spread = spread3[:child_rows] + spread3[child_rows : 2 * child_rows] + spread3[2 * child_rows :]
        stacked = jnp.concatenate(pieces(spread), axis=0)
        front[:, first:last] = front[:, first:last] + dot(landed3, stacked, ((0,), (0,)))

    assemble(0, PANEL)
    pan_copies = [
        pltpu.make_async_remote_copy(
            src_ref=front.at[:, pl.ds(0, PANEL)], dst_ref=panel, send_sem=pan_send.at[step - 1], recv_sem=pan_recv,
            device_id=(row, step), device_id_type=MESH)
        for step in range(1, ncols)
    ]

    @pl.when(col == 0)
    def _():
        for copy in pan_copies:
            copy.start()
        panel[...] = front[:, :PANEL]

    assemble(PANEL, cols_dev)

    @pl.when(col == 0)
    def _():
        for copy in pan_copies:
            copy.wait_send()

    @pl.when(col != 0)
    def _():
        pan_copies[0].wait_recv()

    block_panel = panel[...]
    trans = ((0,), (0,))
    gram[...] = dot_full(block_panel, block_panel, trans)

    chunks = min(n, PANEL // SUBLANES)
    chunk = PANEL // chunks
    own_chunk = lax.rem(row, chunks)
    own_rows = pl.ds(pl.multiple_of(own_chunk * chunk, SUBLANES), chunk)
    gathers = []
    for step in range(1, n):
        peer = lax.rem(row + step, n)
        start = pl.multiple_of(lax.rem(peer, chunks) * chunk, SUBLANES)
        copy = pltpu.make_async_remote_copy(
            src_ref=gram.at[pl.ds(start, chunk)], dst_ref=gram_in.at[row],
            send_sem=gram_send.at[step], recv_sem=gram_recv.at[step], device_id=(peer, col), device_id_type=MESH)
        copy.start()
        gathers.append(copy)
    gram_in[row] = gram[own_rows, :]

    def products(first, last):
        split = min(max(first, cols_dev), last)
        if split > first:
            prod[:, first:split] = dot_full(block_panel, front[:, first:split], trans)
        if last > split:
            prod[:, split:last] = dot_full(block_panel, sides[:, split - cols_dev : last - cols_dev], trans)

    keep_copies = [
        pltpu.make_async_copy(front, front_out, out_sem.at[0]),
        pltpu.make_async_copy(panel, panel_out, out_sem.at[1]),
    ]
    for copy in keep_copies:
        copy.start()

    starts, parts, halving = plan(n, prod.shape[1])
    base = [row * 0] * len(parts)
    nstages = len(parts[0][0])

    def own_bit(bit):
        return (row // (1 << bit)) % 2

    def members(bits):
        mine = sum(own_bit(bit) * (1 << i) for i, bit in enumerate(bits))
        others = []
        for d in range(1, 1 << len(bits)):
            code, peer = 0, row
            for i, bit in enumerate(bits):
                own = own_bit(bit)
                flip = d >> i & 1
                code = code + (1 - own if flip else own) * (1 << i)
                peer = peer + ((1 - 2 * own) * (1 << bit) if flip else 0)
            others.append((code, peer))
        return mine, others

    def send_part(q, stage, at, slot, size, split):
        groups, extras = parts[q]
        bits = groups[stage] if split else extras[stage]
        mine, others = members(bits)
        piece = size >> len(bits) if split else size
        keep = pl.multiple_of(base[q] + mine * piece if split else base[q], SUBLANES)
        width = starts[q + 1] - starts[q]
        sent = []
        for d, (code, peer) in enumerate(others):
            give = pl.multiple_of(base[q] + code * piece, SUBLANES) if split else keep
            copy = pltpu.make_async_remote_copy(
                src_ref=prod.at[pl.ds(give, piece), pl.ds(starts[q], width)],
                dst_ref=halves.at[q, pl.ds(at + d * piece, piece), pl.ds(0, width)],
                send_sem=red_send.at[q, slot + d], recv_sem=red_recv.at[q, slot + d],
                device_id=(peer, col), device_id_type=MESH)
            copy.start()
            sent.append((copy, at + d * piece))
        base[q] = keep
        return sent, keep, piece, width

    def send_stage(stage, at, slot, size, split, before):
        held = []
        for q in range(len(parts)):
            before(q)
            if split:
                marks[q].append(base[q])
            held.append(send_part(q, stage, at, slot, size, split))
        used, piece = len(held[0][0]), held[0][2]
        return held, at + used * piece, slot + used, piece

    def adder(held):
        def add_part(q):
            sent, keep, piece, width = held[q]
            for copy, _ in sent:
                copy.wait()
            spot = (pl.ds(keep, piece), slice(starts[q], starts[q + 1]))
            value = prod[spot]
            for _, at in sent:
                value = value + halves[q, at : at + piece, :width]
            prod[spot] = value

        return add_part

    def share_part(q, stage, slot, piece):
        _, others = members(parts[q][0][stage])
        keep = pl.multiple_of(base[q], SUBLANES)
        spot = total.at[pl.ds(keep, piece), pl.ds(starts[q], starts[q + 1] - starts[q])]
        sent = []
        for d, (_, peer) in enumerate(others):
            copy = pltpu.make_async_remote_copy(
                src_ref=spot, dst_ref=spot, send_sem=red_send.at[q, slot + d], recv_sem=red_recv.at[q, slot + d],
                device_id=(peer, col), device_id_type=MESH)
            copy.start()
            sent.append(copy)
        return sent

    marks = [[] for _ in parts]
    at, slot, size = 0, 0, PANEL
    held, at, slot, size = send_stage(0, at, slot, size, True, lambda q: products(starts[q], starts[q + 1]))

    for copy in gathers:
        copy.wait()
    summed = gram_in[0]
    for k in range(1, n):
        summed = summed + gram_in[k]
    gram_all[own_rows, :] = summed
    spreads = []
    for step in range(1, chunks):
        peer = row - own_chunk + lax.rem(own_chunk + step, chunks)
        copy = pltpu.make_async_remote_copy(
            src_ref=gram_all.at[own_rows], dst_ref=gram_all.at[own_rows],
            send_sem=gram_send.at[n + step], recv_sem=gram_recv.at[n + step],
            device_id=(peer, col), device_id_type=MESH)
        copy.start()
        spreads.append(copy)

    for stage in range(1, nstages):
        held, at, slot, size = send_stage(stage, at, slot, size, True, adder(held))
    for copy in spreads:
        copy.wait()
    turns = PANEL // SUBLANES
    mat, done = gram_all[...], 0

    def turn_by(mat, done, share):
        upto = min(turns, done + share)
        return (sweep_groups(mat, upto - done) if upto > done else mat), upto

    mat, done = turn_by(mat, done, 3)
    for stage in range(len(parts[0][1])):
        held, at, slot, size = send_stage(stage, at, slot, size, False, adder(held))
    last_add = adder(held)
    waiting = [[] for _ in parts]
    for stage in reversed(range(nstages)):
        for q in range(len(parts)):
            if stage == nstages - 1:
                last_add(q)
                spot = (pl.ds(pl.multiple_of(base[q], SUBLANES), size), slice(starts[q], starts[q + 1]))
                total[spot] = prod[spot]
            for copy in waiting[q]:
                copy.wait()
            waiting[q] = share_part(q, stage, slot, size)
            base[q] = marks[q][stage]
        slot += len(waiting[0])
        mat, done = turn_by(mat, done, turns if stage == 0 else 4)
        size <<= len(parts[0][0][stage])

    inverse = -mat
    for q in range(len(parts)):
        for copy in waiting[q]:
            copy.wait()
        first, last = starts[q], starts[q + 1]
        split = min(max(first, cols_dev), last)
        if split > first:
            coefs[:, first:split] = dot_full(inverse, total[:, first:split])
            copy = pltpu.make_async_copy(
                coefs.at[:, pl.ds(first, split - first)], coefs_out.at[:, pl.ds(first, split - first)], out_sem.at[2 + q])
            copy.start()
            keep_copies.append(copy)
        if last > split:
            side[:, split - cols_dev : last - cols_dev] = dot_full(inverse, total[:, split:last])
    copy = pltpu.make_async_copy(side, side_out, out_sem.at[2 + len(parts)])
    copy.start()
    keep_copies.append(copy)
    for copy in keep_copies:
        copy.wait()


def finish(front_hbm, panel_hbm, coefs_hbm, side_hbm, rhs_hbm, updated, side_t, left_t,
           front, panel, coefs, side, rhs_t, stage, in_sem, sems):
    nrhs = rhs_t.shape[0]
    tile = stage.shape[2]
    loads = [
        pltpu.make_async_copy(source, target, in_sem.at[k])
        for k, (source, target) in enumerate(
            [(panel_hbm, panel), (coefs_hbm, coefs), (front_hbm, front), (side_hbm, side), (rhs_hbm, rhs_t)])
    ]
    for load in loads:
        load.start()
    loads[0].wait()
    high, low, _ = pieces(panel[...])
    left = jnp.concatenate([high, high, low], axis=1)

    def product(right):
        top, rest, _ = pieces(right)
        return dot(left, jnp.concatenate([top, rest, top], axis=0), ((1,), (0,)))

    for load in loads[1:]:
        load.wait()
    copies = []
    for t in range(stage.shape[0]):
        at = slice(t * tile, (t + 1) * tile)
        stage[t] = front[:, at] - product(coefs[:, at])
        copy = pltpu.make_async_copy(stage.at[t], updated.at[:, pl.ds(t * tile, tile)], sems.at[t])
        copy.start()
        copies.append(copy)
    sides = side[...]
    side_t[...] = jnp.transpose(sides)[:nrhs]
    left_t[...] = rhs_t[...] - jnp.transpose(product(sides))[:nrhs]
    for copy in copies:
        copy.wait()


def solution(mesh):
    n, ncols = mesh.shape["rows"], mesh.shape["cols"]

    def shards(parent_front, right_sides, child_values, block_owner, row_map, col_map):
        rows_dev, cols_dev = parent_front.shape
        child_rows, child_cols = child_values.shape
        nrhs = right_sides.shape[1]
        side_width = -(-nrhs // LANES) * LANES
        width = cols_dev + side_width
        starts, parts, _ = plan(n, width)
        nparts = len(parts)
        widest = max(starts[q + 1] - starts[q] for q in range(nparts))
        landing_rows, slots = slots_of(n)
        block = child_rows // n
        chunks = min(n, PANEL // SUBLANES)
        vmem = pl.BlockSpec(memory_space=pltpu.VMEM)
        dma = pltpu.SemaphoreType.DMA
        hbm = pl.BlockSpec(memory_space=pltpu.HBM)
        rhs_t = right_sides.T
        front, panel, coefs, side = pl.pallas_call(
            functools.partial(kernel, n, ncols),
            out_shape=(
                jax.ShapeDtypeStruct((rows_dev, cols_dev), f32),
                jax.ShapeDtypeStruct((rows_dev, PANEL), f32),
                jax.ShapeDtypeStruct((PANEL, cols_dev), f32),
                jax.ShapeDtypeStruct((PANEL, side_width), f32),
            ),
            in_specs=[hbm] * 6,
            out_specs=(hbm, hbm, hbm, hbm),
            scratch_shapes=[
                pltpu.VMEM((rows_dev, cols_dev), f32),
                pltpu.VMEM((rows_dev, PANEL), f32),
                pltpu.VMEM((PANEL, cols_dev), f32),
                pltpu.VMEM((PANEL, side_width), f32),
                dma((3 + nparts,)),
                pltpu.SMEM(block_owner.shape, jnp.int32),
                pltpu.VMEM((nrhs, rows_dev), f32),
                pltpu.VMEM((1, child_rows), jnp.int32),
                pltpu.VMEM((1, child_cols), jnp.int32),
                pltpu.VMEM((child_rows, child_cols), f32),
                pltpu.VMEM((n, block, child_cols + LANES), f32),
                pltpu.VMEM((n, block, child_cols + LANES), f32),
                pltpu.VMEM((child_rows, child_cols + LANES), f32),
                pltpu.VMEM((cols_dev, child_cols), bf16),
                pltpu.VMEM((rows_dev, side_width), f32),
                pltpu.VMEM((PANEL, width), f32),
                pltpu.VMEM((PANEL, width), f32),
                pltpu.VMEM((nparts, landing_rows, widest), f32),
                pltpu.VMEM((PANEL, PANEL), f32),
                pltpu.VMEM((n, PANEL // chunks, PANEL), f32),
                pltpu.VMEM((PANEL, PANEL), f32),
                dma((6,)),
                dma((n,)),
                dma((n,)),
                dma((max(ncols - 1, 1),)),
                dma,
                dma((n + chunks,)),
                dma((n + chunks,)),
                dma((nparts, 2 * slots)),
                dma((nparts, 2 * slots)),
            ],
            compiler_params=pltpu.CompilerParams(collective_id=0, has_side_effects=True, vmem_limit_bytes=VMEM_LIMIT),
        )(block_owner, parent_front, rhs_t, child_values, row_map.reshape(1, -1), col_map.reshape(1, -1))
        tile = min(TILE, cols_dev)
        updated, side_t, left_t = pl.pallas_call(
            finish,
            out_shape=(
                jax.ShapeDtypeStruct((rows_dev, cols_dev), f32),
                jax.ShapeDtypeStruct((nrhs, PANEL), f32),
                jax.ShapeDtypeStruct((nrhs, rows_dev), f32),
            ),
            in_specs=[hbm] * 5,
            out_specs=(hbm, vmem, vmem),
            scratch_shapes=[
                pltpu.VMEM((rows_dev, cols_dev), f32),
                pltpu.VMEM((rows_dev, PANEL), f32),
                pltpu.VMEM((PANEL, cols_dev), f32),
                pltpu.VMEM((PANEL, side_width), f32),
                pltpu.VMEM((nrhs, rows_dev), f32),
                pltpu.VMEM((cols_dev // tile, rows_dev, tile), f32),
                dma((5,)),
                dma((cols_dev // tile,)),
            ],
            compiler_params=pltpu.CompilerParams(vmem_limit_bytes=VMEM_LIMIT),
        )(front, panel, coefs, side, rhs_t)
        return updated, side_t.T, left_t.T

    in_specs = (
        P("rows", "cols"),
        P("rows", None),
        P("rows", "cols"),
        P("rows"),
        P("rows"),
        P("cols"),
    )
    out_specs = (P("rows", "cols"), P(), P("rows", None))
    return jax.shard_map(shards, mesh=mesh, in_specs=in_specs, out_specs=out_specs, check_vma=False)
```
